512 devices in a mesh: sky: 64 (over x, z, core), exp: 8 (over y).
Axes of the slice: x: 4, y: 8, z: 8, core: 2. Of those that a mesh axis runs over, the one named last changes fastest.
Arguments:
- padded_tiles: bfloat16 [24576, 10752], P(('sky', 'exp')), may hold values from -6 to 6
- coefficients: float32 [24576, 20], P(('sky', 'exp')), may hold values from -1.8 to 1.8
- row_taps: bfloat16 [24576, 6, 24], P(('sky', 'exp')), may hold values from 0.019897461 to 0.34960938
- col_taps: bfloat16 [24576, 6, 128], P(('sky', 'exp')), may hold values from 0.019897461 to 0.34960938
- shifts: int32 [24576, 2], P(('sky', 'exp')), may hold values from 0 to 2
- mask_words: int32 [24576], P(('sky', 'exp')), may hold values from -2147483648 to 2147483646
- weights: bfloat16 [24576], P(('sky', 'exp')), may hold values from 0.049804688 to 0.5
- destination: int32 [24576, 1], P(('sky', 'exp')), may hold values from 0 to 63; in each aligned block of 48 rows (0 to 47, 48 to 95, ...) at most 2 rows name the same one
- patch_slot: int32 [24576], P(('sky', 'exp')), may hold values from 0 to 15
- basis_rows: bfloat16 [20, 41], replicated, may hold values from -1 to 1
- basis_cols: bfloat16 [20, 41], replicated, may hold values from -1 to 1
Outputs:
- coadd: float32 [24576, 128], P(('sky', 'exp'))
The draws below stay inside these ranges and needn't reach their ends.
Inputs may be any that keep to these rules, and one draw needn't show every extreme that they name: `destination`: the 48 tiles of one device name one patch at most 2 times, a bound that some block reaches.
All inputs are finite; a program needn't handle non-finite values.
Results may differ from the reference program's by a relative error of at most 0.014.
Values may be sent and summed in bfloat16 or wider, within the bound.
No kernel may reach another device: no remote copies, remote signals or barrier semaphores. Data moves between devices by JAX's collectives and lax.ppermute only.
A program may use at most 64 MiB of HBM per device.

```python
import math
import jax
import jax.numpy as jnp
import numpy as np
from jax import lax

NB = 20
KW = 41
TR = 24
TC = 128
BW = 6
SLOTS = 16
TILES_DEV = 48
CAP = 2
TILES = 24576
N_SKY = 64
N_EXP = 8


def set_ends(values, own_key, smallest, largest):
    longest = values.shape.index(max(values.shape))
    spots = []
    for shift in (0, 1):
        where = [jax.random.randint(jax.random.fold_in(own_key, axis), (), 0, length) for axis, length in enumerate(values.shape)]
        where[longest] = (where[longest] + shift) % values.shape[longest]
        spots.append(tuple(where))
    return values.at[spots[0]].set(smallest).at[spots[1]].set(largest)


def shard_levels(rng, dims, split, smallest, largest):
    loudness, own = 1.0, jax.random.fold_in(rng, 6)
    for position, blocks in split:
        heights = jnp.exp(jax.random.uniform(jax.random.fold_in(own, position), (blocks,), jnp.float32, smallest / len(split), largest / len(split)))
        loudness = loudness * jnp.repeat(heights, dims[position] // blocks).reshape([-1 if axis == position else 1 for axis in range(len(dims))])
    return loudness


def deal_out(key, own, number, rows, number_of, top, bound, lean):
    order = jax.random.permutation(key, number_of)
    crowded, usual = shares(number_of, rows * top, bound, lean, True), shares(number_of, rows * top, bound, lean, False)
    places = jnp.arange(number_of)

    def named(sizes, turn):
        used = int((sizes > 0).sum())
        fixed = max(1, used // 4)
        shifted = fixed + (places - fixed + turn * (used - fixed)) % max(1, number_of - fixed)
        return jnp.zeros((number_of,), jnp.int32).at[order[jnp.where(places < fixed, places, shifted)]].set(jnp.asarray(sizes, jnp.int32))

    sizes = jnp.where(number % 4 == 0, named(crowded, number // 4), named(usual, number - number // 4 - 1))
    mixed = jax.random.permutation(jax.random.fold_in(own, 3), number_of)
    donor, sink = mixed[0:number_of // 2 * 2:2], mixed[1:number_of // 2 * 2:2]
    room = jnp.minimum(sizes[donor] - 1, bound - sizes[sink]) // 2
    room = jnp.where((donor == order[0]) | (sink == order[0]) | (sizes[sink] == 0), 0, jnp.maximum(room, 0))
    shifted = jax.random.randint(jax.random.fold_in(own, 4), (number_of // 2,), 0, 1 << 20) % (room + 1)
    sizes = sizes.at[donor].add(-shifted).at[sink].add(shifted)
    items = jnp.searchsorted(jnp.cumsum(sizes), jnp.arange(rows * top), side="right").astype(jnp.int32)
    listing = items.reshape(top, rows).T
    listing = listing[jax.random.permutation(jax.random.fold_in(own, 1), rows)]
    turn = jax.random.randint(jax.random.fold_in(own, 2), (rows, 1), 0, top)
    return jnp.take_along_axis(listing, (jnp.arange(top)[None, :] + turn) % top, axis=1)


def shares(count, total, limit, skew, full):
    loads = [(1 << 20) // math.isqrt(standing ** skew) + 1 for standing in range(1, count + 1)]
    largest = limit if full else min(limit, max(-(-total // count), total * loads[0] // sum(loads)))
    least = 1 if total - largest >= count - 1 else 0
    given, rest = [largest] + [least] * (count - 1), total - largest - least * (count - 1)
    while rest > 0:
        movable = [i for i in range(1, count) if given[i] < largest] or [i for i in range(1, count) if given[i] < limit]
        pool, budget = sum([loads[i] for i in movable]), rest
        for i in movable:
            extra = min(limit - given[i], max(1, budget * loads[i] // pool), rest)
            given[i] = given[i] + extra
            rest = rest - extra
    return np.array(given)


def noise(own_key, extent, spread, bound, shards=(), kind=jnp.bfloat16):
    level = shard_levels(own_key, extent, shards, -0.22, 0.18) if shards else 1.0
    result = jax.random.normal(own_key, extent, jnp.float32) * spread * level
    return jnp.minimum(jnp.maximum(result, -bound), bound).astype(kind)


def setup_inputs(seed: int = 0) -> dict:
    streams_of = jax.random.split(jax.random.key(seed), 12)
    padded_tiles = noise(streams_of[0], (TILES, (TR + KW - 1) * (TC + KW - 1)), 1.0, 6.0, ((0, 512),))
    coefficients = noise(streams_of[1], (TILES, NB), 0.3, 1.8, ((0, 512),), jnp.float32)
    row_taps = jnp.clip(0.019897461 + 0.3297119 * jax.random.uniform(streams_of[2], (TILES, BW, TR), jnp.float32) ** shard_levels(streams_of[2], (TILES, BW, TR), ((0, 512),), -0.2, 0.2), 0.019897461, 0.34960938).astype(jnp.bfloat16)
    col_taps = jnp.clip(0.019897461 + 0.3297119 * jax.random.uniform(streams_of[3], (TILES, BW, TC), jnp.float32) ** shard_levels(streams_of[3], (TILES, BW, TC), ((0, 512),), -0.2, 0.2), 0.019897461, 0.34960938).astype(jnp.bfloat16)
    shifts = set_ends(jax.random.randint(streams_of[4], (TILES, 2), 0, 3), jax.random.fold_in(streams_of[4], 1), 0, 2).astype(jnp.int32)
    mask_words = set_ends(jax.random.randint(streams_of[5], (TILES,), -2147483648, 2147483647), jax.random.fold_in(streams_of[5], 1), -2147483648, 2147483646).astype(jnp.int32)
    weights = jnp.clip(jnp.exp(math.log(0.5) - 2.306499 * jax.random.uniform(streams_of[6], (TILES,), jnp.float32) ** shard_levels(streams_of[6], (TILES,), ((0, 512),), -0.2, 0.2)), 0.049804688, 0.5).astype(jnp.bfloat16)
    destination_keys = jax.random.split(jax.random.fold_in(streams_of[7], 1), TILES // TILES_DEV)
    destination_turns = jax.random.permutation(jax.random.fold_in(streams_of[7], 3), TILES // TILES_DEV)
    destination = jax.vmap(lambda own, number: deal_out(jax.random.fold_in(streams_of[7], 2), own, number, TILES_DEV, N_SKY, 1, CAP, 2))(destination_keys, destination_turns).reshape((TILES, 1))
    patch_slot = set_ends(jax.random.randint(streams_of[8], (TILES,), 0, SLOTS), jax.random.fold_in(streams_of[8], 1), 0, SLOTS - 1).astype(jnp.int32)
    basis_rows = noise(streams_of[9], (NB, KW), KW ** -0.5, 1.0)
    basis_cols = noise(streams_of[10], (NB, KW), KW ** -0.5, 1.0)
    return {"padded_tiles": padded_tiles, "coefficients": coefficients, "row_taps": row_taps, "col_taps": col_taps, "shifts": shifts, "mask_words": mask_words, "weights": weights, "destination": destination, "patch_slot": patch_slot, "basis_rows": basis_rows, "basis_cols": basis_cols}


def toeplitz(basis_vals, distance):
    kernel_len = basis_vals.shape[1]
    picks = (distance[:, :, None] == jnp.arange(kernel_len, dtype=jnp.int32)[None, None, :]).astype(jnp.float32)
    return jnp.einsum('xyk,bk->bxy', picks, basis_vals.astype(jnp.float32)).astype(jnp.bfloat16)


def build_tables(basis_rows, basis_cols, tile_rows, tile_cols):
    kernel_len = basis_rows.shape[1]
    out_rows = jnp.arange(tile_rows, dtype=jnp.int32)
    in_rows = jnp.arange(tile_rows + kernel_len - 1, dtype=jnp.int32)
    out_cols = jnp.arange(tile_cols, dtype=jnp.int32)
    in_cols = jnp.arange(tile_cols + kernel_len - 1, dtype=jnp.int32)
    row_toeplitz = toeplitz(basis_rows, in_rows[None, :] - out_rows[:, None])
    col_toeplitz = toeplitz(basis_cols, in_cols[:, None] - out_cols[None, :])
    return row_toeplitz, col_toeplitz


def band_matrix(tap_values, band_shift):
    tap_count = tap_values.shape[1]
    length = tap_values.shape[2]
    positions = jnp.arange(length, dtype=jnp.int32)
    band_start = jnp.clip(positions[None, :] + band_shift[:, None] - tap_count // 2, 0, length - tap_count)
    band_offset = positions[None, None, :] - band_start[:, :, None]
    matrix = jnp.zeros((tap_values.shape[0], length, length), tap_values.dtype)
    for tap_index in range(tap_count):
        matrix = matrix + jnp.where(band_offset == tap_index, tap_values[:, tap_index, :][:, :, None], jnp.zeros((), tap_values.dtype))
    return matrix


def mask_good(mask_words, tile_rows, tile_cols):
    bit_index = jnp.arange(32, dtype=jnp.int32)
    flagged = jnp.bitwise_and(jnp.right_shift(mask_words[:, None], bit_index[None, :]), 1)
    good_cells = (1 - flagged).astype(jnp.float32).reshape(mask_words.shape[0], 4, 8)
    good_cells = jnp.repeat(good_cells, tile_rows // 4, axis=1)
    return jnp.repeat(good_cells, tile_cols // 8, axis=2)


def match_and_warp(padded, coefficients, row_taps, col_taps, shifts, row_toeplitz, col_toeplitz):
    row_pass = jnp.einsum('bic,ncj->nbij', row_toeplitz.astype(jnp.float32), padded.astype(jnp.float32))
    scaled = (row_pass * coefficients[:, :, None, None]).astype(jnp.bfloat16)
    matched = jnp.einsum('nbij,bjk->nik', scaled.astype(jnp.float32), col_toeplitz.astype(jnp.float32)).astype(jnp.bfloat16)
    row_warp = band_matrix(row_taps, shifts[:, 0])
    col_warp = band_matrix(col_taps, shifts[:, 1])
    halfway = jnp.einsum('nij,njk->nik', row_warp.astype(jnp.float32), matched.astype(jnp.float32)).astype(jnp.bfloat16)
    return jnp.einsum('nij,nkj->nik', halfway.astype(jnp.float32), col_warp.astype(jnp.float32)).astype(jnp.bfloat16)


def reference(padded_tiles, coefficients, row_taps, col_taps, shifts, mask_words, weights, destination, patch_slot, basis_rows, basis_cols):
    row_toeplitz, col_toeplitz = build_tables(basis_rows, basis_cols, TR, TC)
    block_count = N_SKY * N_EXP
    inputs = (padded_tiles, coefficients, row_taps, col_taps, shifts, mask_words, weights, destination, patch_slot)
    grouped = tuple(arr.reshape((block_count, TILES_DEV) + arr.shape[1:]) for arr in inputs)

    def accumulate(state_pair, tile_group):
        numerator, weight_sum = state_pair
        padded, coef_block, rtap, ctap, shift_block, words, weight_block, dest_block, slot_block = tile_group
        padded = padded.reshape(TILES_DEV, TR + KW - 1, TC + KW - 1)
        warped = match_and_warp(padded, coef_block, rtap, ctap, shift_block, row_toeplitz, col_toeplitz)
        good_cells = mask_good(words, TR, TC)
        weight_plane = (weight_block.astype(jnp.float32)[:, None, None] * good_cells).astype(jnp.bfloat16)
        products = weight_plane.astype(jnp.float32) * warped.astype(jnp.float32)
        target = (dest_block[:, 0] * SLOTS + slot_block).astype(jnp.int32)
        numerator = numerator.at[target].add(products)
        weight_sum = weight_sum.at[target].add(weight_plane.astype(jnp.float32))
        return (numerator, weight_sum), None

    zeros_init = jnp.zeros((N_SKY * SLOTS, TR, TC), jnp.float32)
    (numerator, weight_sum), _ = lax.scan(accumulate, (zeros_init, zeros_init), grouped)
    coadd = numerator / jnp.maximum(weight_sum, 1.0)
    return coadd.reshape(N_SKY * SLOTS * TR, TC)
```

```python
import jax
import jax.numpy as jnp
from jax import lax
from jax.sharding import PartitionSpec as P

SLOTS = 16


def toeplitz(basis_vals, distance):
    kernel_len = basis_vals.shape[1]
    picks = (distance[:, :, None] == jnp.arange(kernel_len, dtype=jnp.int32)[None, None, :]).astype(
        jnp.float32
    )
    return jnp.einsum("xyk,bk->bxy", picks, basis_vals.astype(jnp.float32)).astype(jnp.bfloat16)


def build_tables(basis_rows, basis_cols, tile_rows, tile_cols):
    kernel_len = basis_rows.shape[1]
    out_rows = jnp.arange(tile_rows, dtype=jnp.int32)
    in_rows = jnp.arange(tile_rows + kernel_len - 1, dtype=jnp.int32)
    out_cols = jnp.arange(tile_cols, dtype=jnp.int32)
    in_cols = jnp.arange(tile_cols + kernel_len - 1, dtype=jnp.int32)
    row_toeplitz = toeplitz(basis_rows, in_rows[None, :] - out_rows[:, None])
    col_toeplitz = toeplitz(basis_cols, in_cols[:, None] - out_cols[None, :])
    return (row_toeplitz, col_toeplitz)


def band_matrix(tap_values, band_shift):
    tap_count = tap_values.shape[1]
    length = tap_values.shape[2]
    positions = jnp.arange(length, dtype=jnp.int32)
    band_start = jnp.clip(
        positions[None, :] + band_shift[:, None] - tap_count // 2, 0, length - tap_count
    )
    band_offset = positions[None, None, :] - band_start[:, :, None]
    matrix = jnp.zeros((tap_values.shape[0], length, length), tap_values.dtype)
    for tap_index in range(tap_count):
        matrix = matrix + jnp.where(
            band_offset == tap_index,
            tap_values[:, tap_index, :][:, :, None],
            jnp.zeros((), tap_values.dtype),
        )
    return matrix


def spread_cells(cells, tile_rows, tile_cols):
    grid = cells.reshape(cells.shape[0], 4, 8)
    grid = jnp.repeat(grid, tile_rows // 4, axis=1)
    return jnp.repeat(grid, tile_cols // 8, axis=2)


def body(
    padded_tiles,
    coefficients,
    row_taps,
    col_taps,
    shifts,
    mask_words,
    weights,
    destination,
    patch_slot,
    basis_rows,
    basis_cols,
):
    sky_count = lax.axis_size("sky")
    tiles_dev = padded_tiles.shape[0]
    tile_rows = row_taps.shape[2]
    tile_cols = col_taps.shape[2]
    kernel_len = basis_rows.shape[1]
    slot_count = SLOTS
    capacity = 2 * ((tiles_dev + sky_count - 1) // sky_count)
    row_toeplitz, col_toeplitz = build_tables(basis_rows, basis_cols, tile_rows, tile_cols)
    per_block = 8
    block_count = tiles_dev // per_block

    def match_and_warp(tile_group):
        padded, coef_block, rtap, ctap, shift_block = tile_group
        padded = padded.reshape(per_block, tile_rows + kernel_len - 1, tile_cols + kernel_len - 1)
        row_pass = jnp.einsum(
            "bic,ncj->nbij", row_toeplitz, padded, preferred_element_type=jnp.float32
        )
        scaled = (row_pass * coef_block[:, :, None, None]).astype(jnp.bfloat16)
        matched = jnp.einsum(
            "nbij,bjk->nik", scaled, col_toeplitz, preferred_element_type=jnp.float32
        ).astype(jnp.bfloat16)
        row_warp = band_matrix(rtap, shift_block[:, 0])
        col_warp = band_matrix(ctap, shift_block[:, 1])
        halfway = jnp.einsum(
            "nij,njk->nik", row_warp, matched, preferred_element_type=jnp.float32
        ).astype(jnp.bfloat16)
        return jnp.einsum(
            "nij,nkj->nik", halfway, col_warp, preferred_element_type=jnp.float32
        ).astype(jnp.bfloat16)

    inputs = (padded_tiles, coefficients, row_taps, col_taps, shifts)
    grouped = tuple((arr.reshape((block_count, per_block) + arr.shape[1:]) for arr in inputs))
    warped = lax.map(match_and_warp, grouped).reshape(tiles_dev, tile_rows * tile_cols)
    dest_flat = destination[:, 0]
    dest_onehot = (dest_flat[:, None] == jnp.arange(sky_count, dtype=jnp.int32)[None, :]).astype(
        jnp.int32
    )
    before = jnp.cumsum(dest_onehot, axis=0) - dest_onehot
    dest_rank = jnp.sum(before * dest_onehot, axis=1)
    target = dest_flat * capacity + dest_rank
    chosen = jnp.arange(sky_count * capacity, dtype=jnp.int32)[:, None] == target[None, :]
    select = chosen.astype(jnp.bfloat16)
    plane_size = tile_rows * tile_cols
    bit_index = jnp.arange(32, dtype=jnp.int32)
    flagged = jnp.bitwise_and(jnp.right_shift(mask_words[:, None], bit_index[None, :]), 1)
    cell_weights = weights.astype(jnp.float32)[:, None] * (1 - flagged).astype(jnp.float32)
    products = warped.astype(jnp.float32).reshape(tiles_dev, tile_rows, tile_cols) * spread_cells(
        cell_weights, tile_rows, tile_cols
    )
    payload = jnp.concatenate(
        [
            products.reshape(tiles_dev, plane_size).astype(jnp.bfloat16),
            cell_weights.astype(jnp.bfloat16),
            patch_slot[:, None].astype(jnp.bfloat16),
            jnp.zeros((tiles_dev, 128 - 33), jnp.bfloat16),
        ],
        axis=1,
    )
    send = jnp.dot(select, payload, preferred_element_type=jnp.float32).astype(jnp.bfloat16)
    send = send.reshape(sky_count, capacity, plane_size + 128)
    recv = lax.all_to_all(send, "sky", split_axis=0, concat_axis=0, tiled=True)
    recv = recv.reshape(sky_count * capacity, plane_size + 128)
    slot_of = recv[:, plane_size + 32].astype(jnp.int32)
    slot_onehot = (jnp.arange(slot_count, dtype=jnp.int32)[:, None] == slot_of[None, :]).astype(
        jnp.bfloat16
    )
    sums = jnp.dot(slot_onehot, recv, preferred_element_type=jnp.float32).astype(jnp.bfloat16)
    exp_count = lax.axis_size("exp")
    slots_dev = slot_count // exp_count
    sums = sums.reshape(exp_count, slots_dev, plane_size + 128)
    parts = lax.all_to_all(sums, "exp", split_axis=0, concat_axis=0, tiled=True)
    totals = jnp.sum(parts.astype(jnp.float32), axis=0)
    numerator = totals[:, :plane_size].reshape(slots_dev * tile_rows, tile_cols)
    weight_sum = spread_cells(totals[:, plane_size : plane_size + 32], tile_rows, tile_cols)
    return numerator / jnp.maximum(weight_sum.reshape(slots_dev * tile_rows, tile_cols), 1.0)


def solution(mesh):
    placed = (
        P(("sky", "exp"), None),
        P(("sky", "exp"), None),
        P(("sky", "exp"), None, None),
        P(("sky", "exp"), None, None),
        P(("sky", "exp"), None),
        P(("sky", "exp")),
        P(("sky", "exp")),
        P(("sky", "exp"), None),
        P(("sky", "exp")),
        P(),
        P(),
    )
    return jax.shard_map(
        body, mesh=mesh, in_specs=placed, out_specs=P(("sky", "exp"), None), check_vma=False
    )
```

```python
import jax
import jax.numpy as jnp
from jax import lax
from jax.experimental import pallas as pl
from jax.experimental.pallas import tpu as pltpu
from jax.sharding import PartitionSpec as P
F32 = jnp.float32
BF16 = jnp.bfloat16
TRIOS = 16
NB = 20
KW = 41
TR = 24
TC = 128
IR = TR + KW - 1
IC = TC + KW - 1
SPAN = 5


def iota(shape, axis):
    return lax.broadcasted_iota(jnp.int32, shape, axis)


def unpack_tiles(tiles_ref, flat, image):
    for octet in range(6):
        for p in range(84):
            block = tiles_ref[pl.ds(8 * octet, 8), pl.ds(128 * p, 128)].astype(F32)
            flat[pl.ds(8 * octet * 84 + p, 8, stride=84), :] = block
    lane = iota((64, 128), 1)
    for m in range(16):
        first, rest = divmod(IC * m, 128)
        parts = [None] * 4
        for third in range(3):
            shift = (rest - IC * third) % 128
            base = third * 16 * 84 + first
            rolled = {}

            def row(q, rolled=rolled, base=base, shift=shift):
                if q not in rolled:
                    val = flat[pl.ds(base + q, 64, stride=21), :]
                    rolled[q] = pltpu.roll(val, (128 - shift) % 128, 1) if shift else val
                return rolled[q]

            for d in range(4):
                lo, hi = max(128 * d, IC * third), min(128 * d + 128, IC * third + IC)
                if lo >= hi:
                    continue
                start = rest - IC * third + 128 * d
                q0 = start // 128
                edge = 128 - start % 128
                l0, l1 = lo - 128 * d, hi - 128 * d
                if l1 <= edge:
                    val = row(q0)
                elif l0 >= edge:
                    val = row(q0 + 1)
                else:
                    val = jnp.where(lane < edge, row(q0), row(q0 + 1))
                if parts[d] is None:
                    parts[d] = val if l1 == 128 else jnp.where(lane < l1, val, 0.0)
                else:
                    parts[d] = jnp.where(lane < l0, parts[d], val if l1 == 128 else jnp.where(lane < l1, val, 0.0))
        for d in range(4):
            image[pl.ds(d * TRIOS * IR + m, 64, stride=16), :] = parts[d]


def make_tables(brow_ref, bcol_ref, pad, rtab, w0, w1):
    pad[...] = jnp.zeros((32, 128), F32)
    pad[0:NB, 0:KW] = brow_ref[...].astype(F32)
    for b in range(NB):
        line = jnp.broadcast_to(pad[pl.ds(b, 1), :], (TR, 128))
        line = pltpu.roll(line, 0, 1, stride=1, stride_axis=0)
        rtab[pl.ds(b * TR, TR), :] = line
    pad[0:NB, 0:KW] = bcol_ref[...].astype(F32)
    mirror = ((iota((128, 128), 0) + iota((128, 128), 1)) % 128 == 0).astype(BF16)
    rev = jnp.dot(pad[...].astype(BF16), mirror, preferred_element_type=F32)
    pad[...] = rev
    gap = iota((IC, 128), 0) - iota((IC, 128), 1)
    inside = (gap >= 0) & (gap < KW)
    for b in range(NB):
        line = jnp.broadcast_to(pad[pl.ds(b, 1), :], (128, 128))
        line = pltpu.roll(line, 0, 1, stride=1, stride_axis=0)
        band = jnp.concatenate([line, line[: IC - 128]], axis=0)
        band = jnp.where(inside, band, 0.0)
        zero = jnp.zeros((176, 128), F32)
        r = pl.ds(b * 256, 256)
        w0[r, 0:128] = jnp.concatenate([band, zero[:88]], axis=0).astype(BF16)
        w0[r, 128:256] = jnp.concatenate([zero[:168], band[:88]], axis=0).astype(BF16)
        w1[r, 0:128] = jnp.concatenate([band[88:168], zero[:176]], axis=0).astype(BF16)
        w1[r, 128:256] = jnp.concatenate([zero[:80], band, zero[:8]], axis=0).astype(BF16)


def row_stage(image, rtab, coef_s, s0, s1):
    table = rtab[...].astype(BF16)[:, :IR]
    lane = iota((8, 512), 1)

    def step(u, carry):
        halves = []
        for h in range(2):
            n = 2 * u + h
            x = jnp.concatenate(
                [image[pl.ds(pl.multiple_of(d * TRIOS * IR + n * IR, 8), IR), :] for d in range(4)],
                axis=1,
            ).astype(BF16)
            halves.append((n, jnp.dot(table, x, preferred_element_type=F32)))
        for b in range(NB):
            rows = []
            for n, rp in halves:
                scale = jnp.where(
                    lane < IC,
                    coef_s[n, b],
                    jnp.where(lane < 2 * IC, coef_s[n + 16, b], coef_s[n + 32, b]),
                )
                for a in range(3):
                    k = b * TR + 8 * a
                    rows.append(rp[k : k + 8] * scale)
            block = jnp.concatenate(rows, axis=0).astype(BF16)
            at = pl.ds(pl.multiple_of(48 * u, 16), 48)
            s0[at, pl.ds(b * 256, 256)] = block[:, :256]
            s1[at, pl.ds(b * 256, 256)] = block[:, 256:]
        return carry

    lax.fori_loop(0, TRIOS // 2, step, 0)


def column_weights(ctap_ref, shiftv_ref, taps, diag):
    for t in range(48):
        taps[pl.ds(8 * t, 6), :] = ctap_ref[t].astype(F32)
    j = iota((48, 128), 1)
    shift = jnp.broadcast_to(shiftv_ref[:, 1:2], (48, 128))
    offset = jnp.clip(j + shift - 3, 0, TC - 6) - j
    kept = [taps[pl.ds(k, 48, stride=8), :] for k in range(6)]
    for o in range(-SPAN, SPAN + 1):
        total = jnp.zeros((48, 128), F32)
        for k in range(6):
            total = jnp.where(offset + k == o, kept[k], total)
        diag[o + SPAN] = total


def row_weights(rtap_ref, taps):
    taps[...] = jnp.zeros(taps.shape, F32)
    for third in range(3):
        for n in range(TRIOS):
            taps[pl.ds(8 * n, 6), pl.ds(TR * third, TR)] = rtap_ref[n + 16 * third].astype(F32)


def warp_stage(p0, p1, shifts_s, words_s, weights_s, dest_s, slot_s, rowtaps, diag, count, out_ref):
    out_ref[...] = jnp.zeros(out_ref.shape, BF16)

    def clear(d, carry):
        count[d] = 0
        return carry

    lax.fori_loop(0, 64, clear, 0)
    bit = 8 * (iota((TR, 128), 0) // 6) + iota((TR, 128), 1) // 16
    lane8, sub8 = iota((8, 128), 1), iota((8, 128), 0)
    lane1 = iota((1, 128), 1)
    third_of, row_of = lane1 // TR, lane1 % TR
    rr = iota((72, 128), 0)

    def trio(n, carry):
        at = pl.ds(pl.multiple_of(n * TR, 8), TR)
        left, right = p0[at, :], p1[at, :]
        stack = jnp.concatenate(
            [left[:, :128], left[:, 128:] + right[:, :128], right[:, 128:]], axis=0
        ).astype(BF16)
        shift = jnp.where(
            third_of == 0,
            shifts_s[n, 0],
            jnp.where(third_of == 1, shifts_s[n + 16, 0], shifts_s[n + 32, 0]),
        )
        base = third_of * TR + jnp.clip(row_of + shift - 3, 0, TR - 6)
        delta = rr - jnp.broadcast_to(base, (72, 128))
        taps = rowtaps[pl.ds(pl.multiple_of(8 * n, 8), 8), :]
        band = jnp.zeros((72, 128), F32)
        for k in range(6):
            band = jnp.where(delta == k, jnp.broadcast_to(taps[k : k + 1], (72, 128)), band)
        half = lax.dot_general(
            band.astype(BF16), stack, (((0,), (0,)), ((), ())), preferred_element_type=F32
        )
        for third in range(3):
            t = n + 16 * third
            h = half[TR * third : TR * third + TR]
            acc = jnp.zeros((TR, 128), F32)
            for o in range(-SPAN, SPAN + 1):
                d = diag[o + SPAN, pl.ds(t, 1), :]
                moved = pltpu.roll(h, (-o) % 128, 1) if o else h
                acc = acc + jnp.broadcast_to(d, (TR, 128)) * moved
            word, weight = words_s[t], weights_s[t]
            flagged = lax.shift_right_logical(jnp.full((TR, 128), word, jnp.int32), bit) & 1
            prod = (acc * jnp.where(flagged == 0, weight, 0.0)).astype(BF16)
            to = dest_s[t, 0]
            rank = count[to]
            count[to] = rank + 1
            for a in range(3):
                out_ref[to, 3 * rank + a] = prod[8 * a : 8 * a + 8]
            flag8 = lax.shift_right_logical(jnp.full((8, 128), word, jnp.int32), lane8 & 31) & 1
            head = jnp.where(
                lane8 < 32,
                jnp.where(flag8 == 0, weight, 0.0),
                jnp.where(lane8 == 32, jnp.full((8, 128), slot_s[t], jnp.int32).astype(F32), 0.0),
            )
            old = out_ref[to, 6].astype(F32)
            out_ref[to, 6] = jnp.where(sub8 == rank, head, old).astype(BF16)
        return carry

    lax.fori_loop(0, TRIOS, trio, 0)


def send_kernel(
    words_s,
    weights_s,
    dest_s,
    slot_s,
    shifts_s,
    coef_s,
    shiftv_ref,
    tiles_ref,
    rtap_ref,
    ctap_ref,
    brow_ref,
    bcol_ref,
    out_ref,
    flat,
    image,
    pad,
    rtab,
    w0,
    w1,
    s0,
    s1,
    p0,
    p1,
    taps,
    rowtaps,
    diag,
    count,
):
    unpack_tiles(tiles_ref, flat, image)
    make_tables(brow_ref, bcol_ref, pad, rtab, w0, w1)
    column_weights(ctap_ref, shiftv_ref, taps, diag)
    row_weights(rtap_ref, rowtaps)
    row_stage(image, rtab, coef_s, s0, s1)
    p0[...] = jnp.dot(s0[...], w0[...], preferred_element_type=F32)
    p1[...] = jnp.dot(s1[...], w1[...], preferred_element_type=F32)
    warp_stage(
        p0, p1, shifts_s, words_s, weights_s, dest_s, slot_s, rowtaps, diag, count, out_ref
    )


def send_blocks(tiles, coef, rtap, ctap, shifts, words, weights, dest, slot, brow, bcol):
    smem = pl.BlockSpec(memory_space=pltpu.SMEM)
    vmem = pl.BlockSpec(memory_space=pltpu.VMEM)
    return pl.pallas_call(
        send_kernel,
        out_shape=jax.ShapeDtypeStruct((64, 7, 8, 128), BF16),
        in_specs=[smem] * 6 + [vmem] * 6,
        out_specs=vmem,
        scratch_shapes=[
            pltpu.VMEM((48 * 84 + 8, 128), F32),
            pltpu.VMEM((4 * TRIOS * IR, 128), F32),
            pltpu.VMEM((32, 128), F32),
            pltpu.VMEM((NB * TR, 128), F32),
            pltpu.VMEM((NB * 256, 256), BF16),
            pltpu.VMEM((NB * 256, 256), BF16),
            pltpu.VMEM((384, NB * 256), BF16),
            pltpu.VMEM((384, NB * 256), BF16),
            pltpu.VMEM((384, 256), F32),
            pltpu.VMEM((384, 256), F32),
            pltpu.VMEM((48 * 8, 128), F32),
            pltpu.VMEM((TRIOS * 8, 128), F32),
            pltpu.VMEM((2 * SPAN + 1, 48, 128), F32),
            pltpu.SMEM((64,), jnp.int32),
        ],
        compiler_params=pltpu.CompilerParams(vmem_limit_bytes=50 << 20),
        name="match_and_warp",
    )(words, weights.astype(F32), dest, slot, shifts, coef, shifts, tiles, rtap, ctap, brow, bcol)


def body(
    padded_tiles,
    coefficients,
    row_taps,
    col_taps,
    shifts,
    mask_words,
    weights,
    destination,
    patch_slot,
    basis_rows,
    basis_cols,
):
    send = send_blocks(
        padded_tiles,
        coefficients,
        row_taps,
        col_taps,
        shifts,
        mask_words,
        weights,
        destination,
        patch_slot,
        basis_rows,
        basis_cols,
    ).reshape(64, 56, 128)
    recv = lax.all_to_all(send, "sky", split_axis=0, concat_axis=0, tiled=True)
    planes = recv[:, :48].reshape(128, TR * TC)
    heads = recv[:, 48:50].reshape(128, 128)
    slot_of = heads[:, 32].astype(jnp.int32)
    pick = (iota((16, 128), 0) == slot_of[None, :]).astype(BF16)
    sums = jnp.dot(pick, planes, preferred_element_type=F32).astype(BF16)
    cells = jnp.dot(pick, heads, preferred_element_type=F32).astype(BF16)
    parts = jnp.concatenate(
        [sums.reshape(8, 48, 128), cells.reshape(8, 2, 128), jnp.zeros((8, 6, 128), BF16)], axis=1
    )
    parts = lax.all_to_all(parts, "exp", split_axis=0, concat_axis=0, tiled=True)
    totals = jnp.sum(parts.astype(F32), axis=0)
    weight_sum = spread_cells(totals[48:50, :32]).reshape(48, 128)
    return totals[:48] / jnp.maximum(weight_sum, 1.0)


def spread_cells(cells):
    grid = jnp.repeat(cells.reshape(2, 4, 8), TR // 4, axis=1)
    return jnp.repeat(grid, TC // 8, axis=2)


def solution(mesh):
    placed = (
        P(("sky", "exp"), None),
        P(("sky", "exp"), None),
        P(("sky", "exp"), None, None),
        P(("sky", "exp"), None, None),
        P(("sky", "exp"), None),
        P(("sky", "exp")),
        P(("sky", "exp")),
        P(("sky", "exp"), None),
        P(("sky", "exp")),
        P(),
        P(),
    )
    return jax.shard_map(
        body, mesh=mesh, in_specs=placed, out_specs=P(("sky", "exp"), None), check_vma=False
    )
```

```python
import jax
import jax.numpy as jnp
from jax import lax
from jax.experimental import pallas as pl
from jax.experimental.pallas import tpu as pltpu
from jax.sharding import PartitionSpec as P

F32 = jnp.float32
BF16 = jnp.bfloat16
TRIOS = 16
NB = 20
KW = 41
TR = 24
TC = 128
IR = TR + KW - 1
IC = TC + KW - 1
SPAN = 5


def iota(shape, axis):
    return lax.broadcasted_iota(jnp.int32, shape, axis)


def unpack_tiles(tiles_ref, copies, flat, image):
    for octet in range(6):
        copies[octet].wait()
        for p in range(84):
            block = tiles_ref[pl.ds(8 * octet, 8), pl.ds(128 * p, 128)].astype(F32)
            flat[pl.ds(8 * octet * 84 + p, 8, stride=84), :] = block
    lane = iota((64, 128), 1)
    for m in range(16):
        first, rest = divmod(IC * m, 128)
        parts = [None] * 4
        for third in range(3):
            shift = (rest - IC * third) % 128
            base = third * 16 * 84 + first
            rolled = {}

            def row(q, rolled=rolled, base=base, shift=shift):
                if q not in rolled:
                    val = flat[pl.ds(base + q, 64, stride=21), :]
                    rolled[q] = pltpu.roll(val, (128 - shift) % 128, 1) if shift else val
                return rolled[q]

            for d in range(4):
                lo, hi = max(128 * d, IC * third), min(128 * d + 128, IC * third + IC)
                if lo >= hi:
                    continue
                start = rest - IC * third + 128 * d
                q0 = start // 128
                edge = 128 - start % 128
                l0, l1 = lo - 128 * d, hi - 128 * d
                if l1 <= edge:
                    val = row(q0)
                elif l0 >= edge:
                    val = row(q0 + 1)
                else:
                    val = jnp.where(lane < edge, row(q0), row(q0 + 1))
                if parts[d] is None:
                    parts[d] = val if l1 == 128 else jnp.where(lane < l1, val, 0.0)
                else:
                    parts[d] = jnp.where(lane < l0, parts[d], val if l1 == 128 else jnp.where(lane < l1, val, 0.0))
        for d in range(4):
            image[pl.ds(d * TRIOS * IR + m, 64, stride=16), :] = parts[d]


def make_tables(brow_ref, bcol_ref, pad, rtab, w0, w1):
    pad[...] = jnp.zeros((32, 128), F32)
    pad[0:NB, 0:KW] = brow_ref[...].astype(F32)
    for b in range(NB):
        line = jnp.broadcast_to(pad[pl.ds(b, 1), :], (TR, 128))
        line = pltpu.roll(line, 0, 1, stride=1, stride_axis=0)
        rtab[pl.ds(b * TR, TR), :] = line
    pad[0:NB, 0:KW] = bcol_ref[...].astype(F32)
    mirror = ((iota((128, 128), 0) + iota((128, 128), 1)) % 128 == 0).astype(BF16)
    rev = jnp.dot(pad[...].astype(BF16), mirror, preferred_element_type=F32)
    pad[...] = rev
    gap = iota((IC, 128), 0) - iota((IC, 128), 1)
    inside = (gap >= 0) & (gap < KW)
    for b in range(NB):
        line = jnp.broadcast_to(pad[pl.ds(b, 1), :], (128, 128))
        line = pltpu.roll(line, 0, 1, stride=1, stride_axis=0)
        band = jnp.concatenate([line, line[: IC - 128]], axis=0)
        band = jnp.where(inside, band, 0.0)
        zero = jnp.zeros((176, 128), F32)
        r = pl.ds(b * 256, 256)
        w0[r, 0:128] = jnp.concatenate([band, zero[:88]], axis=0).astype(BF16)
        w0[r, 128:256] = jnp.concatenate([zero[:168], band[:88]], axis=0).astype(BF16)
        w1[r, 0:128] = jnp.concatenate([band[88:168], zero[:176]], axis=0).astype(BF16)
        w1[r, 128:256] = jnp.concatenate([zero[:80], band, zero[:8]], axis=0).astype(BF16)


def row_stage(image, rtab, coef_s, s0, s1):
    table = rtab[...].astype(BF16)[:, :IR]
    lane = iota((8, 512), 1)

    def step(u, carry):
        halves = []
        for h in range(2):
            n = 2 * u + h
            x = jnp.concatenate(
                [image[pl.ds(pl.multiple_of(d * TRIOS * IR + n * IR, 8), IR), :] for d in range(4)],
                axis=1,
            ).astype(BF16)
            halves.append((n, jnp.dot(table, x, preferred_element_type=F32)))
        for b in range(NB):
            rows = []
            for n, rp in halves:
                scale = jnp.where(
                    lane < IC,
                    coef_s[b, n],
                    jnp.where(lane < 2 * IC, coef_s[b, n + 16], coef_s[b, n + 32]),
                )
                for a in range(3):
                    k = b * TR + 8 * a
                    rows.append(rp[k : k + 8] * scale)
            block = jnp.concatenate(rows, axis=0).astype(BF16)
            at = pl.ds(pl.multiple_of(48 * u, 16), 48)
            s0[at, pl.ds(b * 256, 256)] = block[:, :256]
            s1[at, pl.ds(b * 256, 256)] = block[:, 256:]
        return carry

    lax.fori_loop(0, TRIOS // 2, step, 0)


def column_weights(ctap_ref, shifts_ref, diag):
    j = iota((48, 128), 1)
    own = jnp.where(
        iota((48, 48), 0) == iota((48, 48), 1),
        jnp.broadcast_to(shifts_ref[1:2, :], (48, 48)).astype(F32),
        0.0,
    )
    shift = jnp.dot(own.astype(BF16), jnp.ones((48, 128), BF16), preferred_element_type=F32)
    offset = jnp.clip(j + shift.astype(jnp.int32) - 3, 0, TC - 6) - j
    kept = [ctap_ref[k].astype(F32) for k in range(6)]
    for o in range(-SPAN, SPAN + 1):
        total = jnp.zeros((48, 128), F32)
        for k in range(6):
            total = jnp.where(offset + k == o, kept[k], total)
        diag[o + SPAN] = total


def row_weights(rtap_ref, rowtaps):
    for k in range(6):
        taps = rtap_ref[k].astype(F32).T
        rowtaps[k] = jnp.concatenate(
            [taps[0:16], taps[16:32], taps[32:48], jnp.zeros((16, 56), F32)], axis=1
        )


def row_warp(p0, p1, shifts_s, rowtaps, half):
    lane1 = iota((1, 128), 1)
    third_of, row_of = lane1 // TR, lane1 % TR
    rr = iota((72, 128), 0)

    def trio(n, carry):
        at = pl.ds(pl.multiple_of(n * TR, 8), TR)
        left, right = p0[at, :], p1[at, :]
        stack = jnp.concatenate(
            [left[:, :128], left[:, 128:] + right[:, :128], right[:, 128:]], axis=0
        ).astype(BF16)
        shift = jnp.where(
            third_of == 0,
            shifts_s[0, n],
            jnp.where(third_of == 1, shifts_s[0, n + 16], shifts_s[0, n + 32]),
        )
        base = third_of * TR + jnp.clip(row_of + shift - 3, 0, TR - 6)
        delta = rr - jnp.broadcast_to(base, (72, 128))
        band = jnp.zeros((72, 128), F32)
        for k in range(6):
            taps = jnp.broadcast_to(rowtaps[k, pl.ds(n, 1), :], (72, 128))
            band = jnp.where(delta == k, taps, band)
        out = lax.dot_general(
            band.astype(BF16), stack, (((0,), (0,)), ((), ())), preferred_element_type=F32
        )
        half[n] = out[:72]
        return carry

    lax.fori_loop(0, TRIOS, trio, 0, unroll=UNROLL_A)


def place_tiles(half, words_s, weights_s, dest_s, slot_s, diag, count, heads, planes_ref):
    bit = 8 * (iota((TR, 128), 0) // 6) + iota((TR, 128), 1) // 16
    lane1 = iota((1, 128), 1)

    def trio(n, carry):
        for third in range(3):
            t = n + 16 * third
            h = half[n, pl.ds(TR * third, TR), :]
            acc = jnp.broadcast_to(diag[SPAN, pl.ds(t, 1), :], (TR, 128)) * h
            for o in range(1, SPAN + 1):
                for sign in (-o, o):
                    d = jnp.broadcast_to(diag[sign + SPAN, pl.ds(t, 1), :], (TR, 128))
                    acc = acc + d * pltpu.roll(h, (-sign) % 128, 1)
            word, weight = words_s[t], weights_s[t]
            flagged = lax.shift_right_logical(jnp.full((TR, 128), word, jnp.int32), bit) & 1
            prod = (acc * jnp.where(flagged == 0, weight, 0.0)).astype(BF16)
            to = dest_s[0, t]
            rank = count[to]
            count[to] = rank + 1
            at = 2 * to + rank
            planes_ref[at] = prod
            flag1 = lax.shift_right_logical(jnp.full((1, 128), word, jnp.int32), lane1 & 31) & 1
            heads[pl.ds(at, 1), :] = jnp.where(
                lane1 < 32,
                jnp.where(flag1 == 0, weight, 0.0),
                jnp.where(lane1 == 32, jnp.full((1, 128), slot_s[t], jnp.int32).astype(F32), 0.0),
            )
        return carry

    lax.fori_loop(0, TRIOS, trio, 0, unroll=UNROLL_B)


def clear_blocks(count, heads, planes_ref):
    planes_ref[...] = jnp.zeros(planes_ref.shape, BF16)
    heads[...] = jnp.zeros(heads.shape, F32)

    def clear(d, carry):
        count[d] = 0
        return carry

    lax.fori_loop(0, 64, clear, 0, unroll=8)


def send_kernel(
    words_s,
    weights_s,
    dest_s,
    slot_s,
    shifts_s,
    coef_s,
    shifts_ref,
    rtap_ref,
    ctap_ref,
    brow_ref,
    bcol_ref,
    tiles_hbm,
    planes_ref,
    heads_ref,
    tiles,
    sems,
    flat,
    image,
    pad,
    rtab,
    w0,
    w1,
    s0,
    s1,
    p0,
    p1,
    rowtaps,
    diag,
    half,
    heads,
    count,
):
    copies = []
    for octet in range(6):
        rows = pl.ds(8 * octet, 8)
        copies.append(
            pltpu.make_async_copy(tiles_hbm.at[rows, :], tiles.at[rows, :], sems.at[octet])
        )
        copies[-1].start()
    make_tables(brow_ref, bcol_ref, pad, rtab, w0, w1)
    column_weights(ctap_ref, shifts_ref, diag)
    row_weights(rtap_ref, rowtaps)
    clear_blocks(count, heads, planes_ref)
    unpack_tiles(tiles, copies, flat, image)
    row_stage(image, rtab, coef_s, s0, s1)
    p0[...] = jnp.dot(s0[...], w0[...], preferred_element_type=F32)
    p1[...] = jnp.dot(s1[...], w1[...], preferred_element_type=F32)
    row_warp(p0, p1, shifts_s, rowtaps, half)
    place_tiles(half, words_s, weights_s, dest_s, slot_s, diag, count, heads, planes_ref)
    heads_ref[...] = heads[...].astype(BF16)


UNROLL_A = 4
UNROLL_B = 2


def send_blocks(tiles, coef, rtap, ctap, shifts, words, weights, dest, slot, brow, bcol):
    smem = pl.BlockSpec(memory_space=pltpu.SMEM)
    vmem = pl.BlockSpec(memory_space=pltpu.VMEM)
    return pl.pallas_call(
        send_kernel,
        out_shape=(
            jax.ShapeDtypeStruct((128, TR, TC), BF16),
            jax.ShapeDtypeStruct((128, 128), BF16),
        ),
        in_specs=[smem] * 6 + [vmem] * 5 + [pl.BlockSpec(memory_space=pltpu.HBM)],
        out_specs=(vmem, vmem),
        scratch_shapes=[
            pltpu.VMEM((48, IR * IC), BF16),
            pltpu.SemaphoreType.DMA((6,)),
            pltpu.VMEM((48 * 84 + 8, 128), F32),
            pltpu.VMEM((4 * TRIOS * IR, 128), F32),
            pltpu.VMEM((32, 128), F32),
            pltpu.VMEM((NB * TR, 128), F32),
            pltpu.VMEM((NB * 256, 256), BF16),
            pltpu.VMEM((NB * 256, 256), BF16),
            pltpu.VMEM((384, NB * 256), BF16),
            pltpu.VMEM((384, NB * 256), BF16),
            pltpu.VMEM((384, 256), F32),
            pltpu.VMEM((384, 256), F32),
            pltpu.VMEM((6, TRIOS, 128), F32),
            pltpu.VMEM((2 * SPAN + 1, 48, 128), F32),
            pltpu.VMEM((TRIOS, 72, 128), F32),
            pltpu.VMEM((128, 128), F32),
            pltpu.SMEM((64,), jnp.int32),
        ],
        compiler_params=pltpu.CompilerParams(vmem_limit_bytes=67043328),
        name="match_and_warp",
    )(
        words,
        weights.astype(F32),
        dest.T,
        slot,
        shifts.T,
        coef.T,
        shifts.T,
        rtap.transpose(1, 2, 0),
        ctap.transpose(1, 0, 2),
        brow,
        bcol,
        tiles,
    )


def body(
    padded_tiles,
    coefficients,
    row_taps,
    col_taps,
    shifts,
    mask_words,
    weights,
    destination,
    patch_slot,
    basis_rows,
    basis_cols,
):
    planes, heads = send_blocks(
        padded_tiles,
        coefficients,
        row_taps,
        col_taps,
        shifts,
        mask_words,
        weights,
        destination,
        patch_slot,
        basis_rows,
        basis_cols,
    )
    send = jnp.concatenate([planes.reshape(64, 2, TR * TC), heads.reshape(64, 2, 128)], axis=2)
    recv = lax.all_to_all(send, "sky", split_axis=0, concat_axis=0, tiled=True)
    recv = recv.reshape(128, TR * TC + 128)
    slot_of = recv[:, TR * TC + 32].astype(jnp.int32)
    pick = (iota((16, 128), 0) == slot_of[None, :]).astype(BF16)
    sums = jnp.dot(pick, recv, preferred_element_type=F32).astype(BF16)
    parts = sums.reshape(8, 2, TR * TC + 128)
    parts = lax.all_to_all(parts, "exp", split_axis=0, concat_axis=0, tiled=True)
    totals = jnp.sum(parts.astype(F32), axis=0)
    numerator = totals[:, : TR * TC].reshape(2 * TR, TC)
    weight_sum = spread_cells(totals[:, TR * TC : TR * TC + 32]).reshape(2 * TR, TC)
    return numerator / jnp.maximum(weight_sum, 1.0)


def spread_cells(cells):
    grid = jnp.repeat(cells.reshape(2, 4, 8), TR // 4, axis=1)
    return jnp.repeat(grid, TC // 8, axis=2)


def solution(mesh):
    placed = (
        P(("sky", "exp"), None),
        P(("sky", "exp"), None),
        P(("sky", "exp"), None, None),
        P(("sky", "exp"), None, None),
        P(("sky", "exp"), None),
        P(("sky", "exp")),
        P(("sky", "exp")),
        P(("sky", "exp"), None),
        P(("sky", "exp")),
        P(),
        P(),
    )
    return jax.shard_map(
        body, mesh=mesh, in_specs=placed, out_specs=P(("sky", "exp"), None), check_vma=False
    )
```

```python
import jax
import jax.numpy as jnp
from jax import lax
from jax.experimental import pallas as pl
from jax.experimental.pallas import tpu as pltpu
from jax.sharding import PartitionSpec as P

F32 = jnp.float32
BF16 = jnp.bfloat16
TRIOS = 16
NB = 20
KW = 41
TR = 24
TC = 128
IR = TR + KW - 1
IC = TC + KW - 1
SPAN = 5
PITCH = 136


def iota(shape, axis):
    return lax.broadcasted_iota(jnp.int32, shape, axis)


def unpack_tiles(tiles_ref, copies, flat, image):
    for octet in range(6):
        copies[octet].wait()
        for p in range(84):
            block = tiles_ref[pl.ds(8 * octet, 8), pl.ds(128 * p, 128)].astype(F32)
            flat[pl.ds(8 * octet * 84 + p, 8, stride=84), :] = block
    lane = iota((64, 128), 1)
    for m in range(16):
        first, rest = divmod(IC * m, 128)
        parts = [None] * 4
        for third in range(3):
            shift = (rest - IC * third) % 128
            base = third * 16 * 84 + first
            rolled = {}

            def row(q, rolled=rolled, base=base, shift=shift):
                if q not in rolled:
                    val = flat[pl.ds(base + q, 64, stride=21), :]
                    rolled[q] = pltpu.roll(val, (128 - shift) % 128, 1) if shift else val
                return rolled[q]

            for d in range(4):
                lo, hi = max(128 * d, IC * third), min(128 * d + 128, IC * third + IC)
                if lo >= hi:
                    continue
                start = rest - IC * third + 128 * d
                q0 = start // 128
                edge = 128 - start % 128
                l0, l1 = lo - 128 * d, hi - 128 * d
                if l1 <= edge:
                    val = row(q0)
                elif l0 >= edge:
                    val = row(q0 + 1)
                else:
                    val = jnp.where(lane < edge, row(q0), row(q0 + 1))
                if parts[d] is None:
                    parts[d] = val if l1 == 128 else jnp.where(lane < l1, val, 0.0)
                else:
                    parts[d] = jnp.where(lane < l0, parts[d], val if l1 == 128 else jnp.where(lane < l1, val, 0.0))
        for d in range(4):
            image[pl.ds(d * TRIOS * IR + m, 64, stride=16), :] = parts[d]


def make_tables(brow_ref, bcol_ref, pad, rtab, w0, w1):
    pad[...] = jnp.zeros((32, 128), F32)
    pad[0:NB, 0:KW] = brow_ref[...].astype(F32)
    for b in range(NB):
        line = jnp.broadcast_to(pad[pl.ds(b, 1), :], (TR, 128))
        line = pltpu.roll(line, 0, 1, stride=1, stride_axis=0)
        rtab[pl.ds(b * TR, TR), :] = line
    pad[0:NB, 0:KW] = bcol_ref[...].astype(F32)
    mirror = ((iota((128, 128), 0) + iota((128, 128), 1)) % 128 == 0).astype(BF16)
    rev = jnp.dot(pad[...].astype(BF16), mirror, preferred_element_type=F32)
    pad[...] = rev
    gap = iota((IC, 128), 0) - iota((IC, 128), 1)
    inside = (gap >= 0) & (gap < KW)
    for b in range(NB):
        line = jnp.broadcast_to(pad[pl.ds(b, 1), :], (128, 128))
        line = pltpu.roll(line, 0, 1, stride=1, stride_axis=0)
        band = jnp.concatenate([line, line[: IC - 128]], axis=0)
        band = jnp.where(inside, band, 0.0)
        zero = jnp.zeros((176, 128), F32)
        r = pl.ds(b * 256, 256)
        w0[r, 0:128] = jnp.concatenate([band, zero[:88]], axis=0).astype(BF16)
        w0[r, 128:256] = jnp.concatenate([zero[:168], band[:88]], axis=0).astype(BF16)
        w1[r, 0:128] = jnp.concatenate([band[88:168], zero[:176]], axis=0).astype(BF16)
        w1[r, 128:256] = jnp.concatenate([zero[:80], band, zero[:8]], axis=0).astype(BF16)


def row_stage(image, rtab, coef_s, s0, s1):
    table = rtab[...].astype(BF16)[:, :IR]
    lane = iota((8, 512), 1)

    def step(u, carry):
        halves = []
        for h in range(2):
            n = 2 * u + h
            x = jnp.concatenate(
                [image[pl.ds(pl.multiple_of(d * TRIOS * IR + n * IR, 8), IR), :] for d in range(4)],
                axis=1,
            ).astype(BF16)
            halves.append((n, jnp.dot(table, x, preferred_element_type=F32)))
        for b in range(NB):
            rows = []
            for n, rp in halves:
                scale = jnp.where(
                    lane < IC,
                    coef_s[b, n],
                    jnp.where(lane < 2 * IC, coef_s[b, n + 16], coef_s[b, n + 32]),
                )
                for a in range(3):
                    k = b * TR + 8 * a
                    rows.append(rp[k : k + 8] * scale)
            block = jnp.concatenate(rows, axis=0).astype(BF16)
            at = pl.ds(pl.multiple_of(48 * u, 16), 48)
            s0[at, pl.ds(b * 256, 256)] = block[:, :256]
            s1[at, pl.ds(b * 256, 256)] = block[:, 256:]
        return carry

    lax.fori_loop(0, TRIOS // 2, step, 0)


def lane_copies(row):
    own = jnp.where(
        iota((48, 48), 0) == iota((48, 48), 1), jnp.broadcast_to(row, (48, 48)), 0.0
    )
    return jnp.dot(own.astype(BF16), jnp.ones((48, 128), BF16), preferred_element_type=F32)


def column_weights(ctap_ref, shifts_ref, weights_ref, diag, tile_weights):
    tile_weights[...] = lane_copies(weights_ref[...].astype(F32))
    j = iota((48, 128), 1)
    shift = lane_copies(shifts_ref[1:2, :].astype(F32))
    offset = jnp.clip(j + shift.astype(jnp.int32) - 3, 0, TC - 6) - j
    kept = [ctap_ref[k].astype(F32) for k in range(6)]
    for o in range(-SPAN, SPAN + 1):
        total = jnp.zeros((48, 128), F32)
        for k in range(6):
            total = jnp.where(offset + k == o, kept[k], total)
        diag[o + SPAN] = total


def row_weights(rtap_ref, rowtaps):
    for k in range(6):
        taps = rtap_ref[k].astype(F32).T
        rowtaps[k] = jnp.concatenate(
            [taps[0:16], taps[16:32], taps[32:48], jnp.zeros((16, 56), F32)], axis=1
        )


def row_warp(p0, p1, shifts_s, rowtaps, half):
    lane1 = iota((1, 128), 1)
    third_of, row_of = lane1 // TR, lane1 % TR
    rr = iota((72, 128), 0)

    def trio(n, carry):
        at = pl.ds(pl.multiple_of(n * TR, 8), TR)
        left, right = p0[at, :], p1[at, :]
        stack = jnp.concatenate(
            [left[:, :128], left[:, 128:] + right[:, :128], right[:, 128:]], axis=0
        ).astype(BF16)
        shift = jnp.where(
            third_of == 0,
            shifts_s[0, n],
            jnp.where(third_of == 1, shifts_s[0, n + 16], shifts_s[0, n + 32]),
        )
        base = third_of * TR + jnp.clip(row_of + shift - 3, 0, TR - 6)
        delta = rr - jnp.broadcast_to(base, (72, 128))
        band = jnp.zeros((72, 128), F32)
        for k in range(6):
            taps = jnp.broadcast_to(rowtaps[k, pl.ds(n, 1), :], (72, 128))
            band = jnp.where(delta == k, taps, band)
        out = lax.dot_general(
            band.astype(BF16), stack, (((0,), (0,)), ((), ())), preferred_element_type=F32
        )
        half[n] = out[:72]
        return carry

    lax.fori_loop(0, TRIOS, trio, 0, unroll=UNROLL_A)


def place_tiles(half, words_s, dest_s, slot_s, diag, tile_weights, count, blocks):
    bit = 8 * (iota((TR, 128), 0) // 6) + iota((TR, 128), 1) // 16
    lane1 = iota((1, 128), 1)

    def trio(n, carry):
        for third in range(3):
            t = n + 16 * third
            h = half[n, pl.ds(TR * third, TR), :]
            acc = jnp.broadcast_to(diag[SPAN, pl.ds(t, 1), :], (TR, 128)) * h
            for o in range(1, SPAN + 1):
                for sign in (-o, o):
                    d = jnp.broadcast_to(diag[sign + SPAN, pl.ds(t, 1), :], (TR, 128))
                    acc = acc + d * pltpu.roll(h, (-sign) % 128, 1)
            word, weight = words_s[t], tile_weights[pl.ds(t, 1), :]
            flagged = lax.shift_right_logical(jnp.full((TR, 128), word, jnp.int32), bit) & 1
            prod = acc * jnp.where(flagged == 0, jnp.broadcast_to(weight, (TR, 128)), 0.0)
            to = dest_s[0, t]
            rank = count[to]
            count[to] = rank + 1
            at = 2 * to + rank
            blocks[pl.ds(at, TR, stride=PITCH), :] = prod
            flag1 = lax.shift_right_logical(jnp.full((1, 128), word, jnp.int32), lane1 & 31) & 1
            blocks[pl.ds(TR * PITCH + at, 1), :] = jnp.where(
                lane1 < 32,
                jnp.where(flag1 == 0, weight, 0.0),
                jnp.where(lane1 == 32, jnp.full((1, 128), slot_s[t], jnp.int32).astype(F32), 0.0),
            )
        return carry

    lax.fori_loop(0, TRIOS, trio, 0, unroll=UNROLL_B)


def clear_blocks(count, blocks):
    blocks[...] = jnp.zeros(blocks.shape, F32)

    def clear(d, carry):
        count[d] = 0
        return carry

    lax.fori_loop(0, 64, clear, 0, unroll=8)


def send_kernel(
    words_s,
    dest_s,
    slot_s,
    shifts_s,
    coef_s,
    shifts_ref,
    weights_ref,
    rtap_ref,
    ctap_ref,
    brow_ref,
    bcol_ref,
    tiles_hbm,
    out_ref,
    tiles,
    sems,
    flat,
    image,
    pad,
    rtab,
    w0,
    w1,
    s0,
    s1,
    p0,
    p1,
    rowtaps,
    diag,
    half,
    tile_weights,
    blocks,
    count,
):
    copies = []
    for octet in range(6):
        rows = pl.ds(8 * octet, 8)
        copies.append(
            pltpu.make_async_copy(tiles_hbm.at[rows, :], tiles.at[rows, :], sems.at[octet])
        )
        copies[-1].start()
    make_tables(brow_ref, bcol_ref, pad, rtab, w0, w1)
    column_weights(ctap_ref, shifts_ref, weights_ref, diag, tile_weights)
    row_weights(rtap_ref, rowtaps)
    clear_blocks(count, blocks)
    unpack_tiles(tiles, copies, flat, image)
    row_stage(image, rtab, coef_s, s0, s1)
    p0[...] = jnp.dot(s0[...], w0[...], preferred_element_type=F32)
    p1[...] = jnp.dot(s1[...], w1[...], preferred_element_type=F32)
    row_warp(p0, p1, shifts_s, rowtaps, half)
    place_tiles(half, words_s, dest_s, slot_s, diag, tile_weights, count, blocks)
    for i in range(TR + 1):
        out_ref[:, pl.ds(128 * i, 128)] = blocks[pl.ds(PITCH * i, 128), :].astype(BF16)


UNROLL_A = 4
UNROLL_B = 2


def send_blocks(tiles, coef, rtap, ctap, shifts, words, weights, dest, slot, brow, bcol):
    smem = pl.BlockSpec(memory_space=pltpu.SMEM)
    vmem = pl.BlockSpec(memory_space=pltpu.VMEM)
    return pl.pallas_call(
        send_kernel,
        out_shape=jax.ShapeDtypeStruct((128, (TR + 1) * 128), BF16),
        in_specs=[smem] * 5 + [vmem] * 6 + [pl.BlockSpec(memory_space=pltpu.HBM)],
        out_specs=vmem,
        scratch_shapes=[
            pltpu.VMEM((48, IR * IC), BF16),
            pltpu.SemaphoreType.DMA((6,)),
            pltpu.VMEM((48 * 84 + 8, 128), F32),
            pltpu.VMEM((4 * TRIOS * IR, 128), F32),
            pltpu.VMEM((32, 128), F32),
            pltpu.VMEM((NB * TR, 128), F32),
            pltpu.VMEM((NB * 256, 256), BF16),
            pltpu.VMEM((NB * 256, 256), BF16),
            pltpu.VMEM((384, NB * 256), BF16),
            pltpu.VMEM((384, NB * 256), BF16),
            pltpu.VMEM((384, 256), F32),
            pltpu.VMEM((384, 256), F32),
            pltpu.VMEM((6, TRIOS, 128), F32),
            pltpu.VMEM((2 * SPAN + 1, 48, 128), F32),
            pltpu.VMEM((TRIOS, 72, 128), F32),
            pltpu.VMEM((48, 128), F32),
            pltpu.VMEM(((TR + 1) * PITCH, 128), F32),
            pltpu.SMEM((64,), jnp.int32),
        ],
        compiler_params=pltpu.CompilerParams(vmem_limit_bytes=67043328),
        name="match_and_warp",
    )(
        words,
        dest.T,
        slot,
        shifts.T,
        coef.T,
        shifts.T,
        weights.reshape(1, 48),
        rtap.transpose(1, 2, 0),
        ctap.transpose(1, 0, 2),
        brow,
        bcol,
        tiles,
    )


def body(
    padded_tiles,
    coefficients,
    row_taps,
    col_taps,
    shifts,
    mask_words,
    weights,
    destination,
    patch_slot,
    basis_rows,
    basis_cols,
):
    blocks = send_blocks(
        padded_tiles,
        coefficients,
        row_taps,
        col_taps,
        shifts,
        mask_words,
        weights,
        destination,
        patch_slot,
        basis_rows,
        basis_cols,
    )
    send = blocks.reshape(64, 2, TR * TC + 128)
    recv = lax.all_to_all(send, "sky", split_axis=0, concat_axis=0, tiled=True)
    recv = recv.reshape(128, TR * TC + 128)
    slot_of = recv[:, TR * TC + 32].astype(jnp.int32)
    pick = (iota((16, 128), 0) == slot_of[None, :]).astype(BF16)
    sums = jnp.dot(pick, recv, preferred_element_type=F32).astype(BF16)
    parts = sums.reshape(8, 2, TR * TC + 128)
    parts = lax.all_to_all(parts, "exp", split_axis=0, concat_axis=0, tiled=True)
    totals = jnp.sum(parts.astype(F32), axis=0)
    numerator = totals[:, : TR * TC].reshape(2 * TR, TC)
    weight_sum = spread_cells(totals[:, TR * TC : TR * TC + 32]).reshape(2 * TR, TC)
    return numerator / jnp.maximum(weight_sum, 1.0)


def spread_cells(cells):
    grid = jnp.repeat(cells.reshape(2, 4, 8), TR // 4, axis=1)
    return jnp.repeat(grid, TC // 8, axis=2)


def solution(mesh):
    placed = (
        P(("sky", "exp"), None),
        P(("sky", "exp"), None),
        P(("sky", "exp"), None, None),
        P(("sky", "exp"), None, None),
        P(("sky", "exp"), None),
        P(("sky", "exp")),
        P(("sky", "exp")),
        P(("sky", "exp"), None),
        P(("sky", "exp")),
        P(),
        P(),
    )
    return jax.shard_map(
        body, mesh=mesh, in_specs=placed, out_specs=P(("sky", "exp"), None), check_vma=False
    )
```

```python
import jax
import jax.numpy as jnp
from jax import lax
from jax.experimental import pallas as pl
from jax.experimental.pallas import tpu as pltpu
from jax.sharding import PartitionSpec as P

F32 = jnp.float32
BF16 = jnp.bfloat16
TRIOS = 16
NB = 20
KW = 41
TR = 24
TC = 128
IR = TR + KW - 1
IC = TC + KW - 1
SPAN = 5
PITCH = 136


def iota(shape, axis):
    return lax.broadcasted_iota(jnp.int32, shape, axis)


def unpack_tiles(tiles_ref, copies, flat, image):
    for octet in range(6):
        copies[octet].wait()
        for p in range(84):
            block = tiles_ref[pl.ds(8 * octet, 8), pl.ds(128 * p, 128)].astype(F32)
            flat[pl.ds(8 * octet * 84 + p, 8, stride=84), :] = block
    lane = iota((64, 128), 1)
    for m in range(16):
        first, rest = divmod(IC * m, 128)
        parts = [None] * 4
        for third in range(3):
            shift = (rest - IC * third) % 128
            base = third * 16 * 84 + first
            rolled = {}

            def row(q, rolled=rolled, base=base, shift=shift):
                if q not in rolled:
                    val = flat[pl.ds(base + q, 64, stride=21), :]
                    rolled[q] = pltpu.roll(val, (128 - shift) % 128, 1) if shift else val
                return rolled[q]

            for d in range(4):
                lo, hi = max(128 * d, IC * third), min(128 * d + 128, IC * third + IC)
                if lo >= hi:
                    continue
                start = rest - IC * third + 128 * d
                q0 = start // 128
                edge = 128 - start % 128
                l0, l1 = lo - 128 * d, hi - 128 * d
                if l1 <= edge:
                    val = row(q0)
                elif l0 >= edge:
                    val = row(q0 + 1)
                else:
                    val = jnp.where(lane < edge, row(q0), row(q0 + 1))
                if parts[d] is None:
                    parts[d] = val if l1 == 128 else jnp.where(lane < l1, val, 0.0)
                else:
                    parts[d] = jnp.where(lane < l0, parts[d], val if l1 == 128 else jnp.where(lane < l1, val, 0.0))
        for d in range(4):
            image[pl.ds(d * TRIOS * IR + m, 64, stride=16), :] = parts[d]


def make_tables(brow_ref, bcol_ref, pad, rtab, w0, w1):
    pad[...] = jnp.zeros((32, 128), F32)
    pad[0:NB, 0:KW] = brow_ref[...].astype(F32)
    for b in range(NB):
        line = jnp.broadcast_to(pad[pl.ds(b, 1), :], (TR, 128))
        line = pltpu.roll(line, 0, 1, stride=1, stride_axis=0)
        rtab[pl.ds(b * TR, TR), :] = line
    pad[0:NB, 0:KW] = bcol_ref[...].astype(F32)
    mirror = ((iota((128, 128), 0) + iota((128, 128), 1)) % 128 == 0).astype(BF16)
    rev = jnp.dot(pad[...].astype(BF16), mirror, preferred_element_type=F32)
    pad[...] = rev
    gap = iota((IC, 128), 0) - iota((IC, 128), 1)
    inside = (gap >= 0) & (gap < KW)
    for b in range(NB):
        line = jnp.broadcast_to(pad[pl.ds(b, 1), :], (128, 128))
        line = pltpu.roll(line, 0, 1, stride=1, stride_axis=0)
        band = jnp.concatenate([line, line[: IC - 128]], axis=0)
        band = jnp.where(inside, band, 0.0)
        zero = jnp.zeros((176, 128), F32)
        r = pl.ds(b * 256, 256)
        w0[r, 0:128] = jnp.concatenate([band, zero[:88]], axis=0).astype(BF16)
        w0[r, 128:256] = jnp.concatenate([zero[:168], band[:88]], axis=0).astype(BF16)
        w1[r, 0:128] = jnp.concatenate([band[88:168], zero[:176]], axis=0).astype(BF16)
        w1[r, 128:256] = jnp.concatenate([zero[:80], band, zero[:8]], axis=0).astype(BF16)


def row_stage(image, rtab, coef_s, s0, s1):
    table = rtab[...].astype(BF16)[:, :IR]
    lane = iota((8, 512), 1)

    def step(u, carry):
        halves = []
        for h in range(2):
            n = 2 * u + h
            x = jnp.concatenate(
                [image[pl.ds(pl.multiple_of(d * TRIOS * IR + n * IR, 8), IR), :] for d in range(4)],
                axis=1,
            ).astype(BF16)
            halves.append((n, jnp.dot(table, x, preferred_element_type=F32)))
        for b in range(NB):
            rows = []
            for n, rp in halves:
                scale = jnp.where(
                    lane < IC,
                    coef_s[b, n],
                    jnp.where(lane < 2 * IC, coef_s[b, n + 16], coef_s[b, n + 32]),
                )
                for a in range(3):
                    k = b * TR + 8 * a
                    rows.append(rp[k : k + 8] * scale)
            block = jnp.concatenate(rows, axis=0).astype(BF16)
            at = pl.ds(pl.multiple_of(48 * u, 16), 48)
            s0[at, pl.ds(b * 256, 256)] = block[:, :256]
            s1[at, pl.ds(b * 256, 256)] = block[:, 256:]
        return carry

    lax.fori_loop(0, TRIOS // 2, step, 0)


def lane_copies(row):
    own = jnp.where(
        iota((48, 48), 0) == iota((48, 48), 1), jnp.broadcast_to(row, (48, 48)), 0.0
    )
    return jnp.dot(own.astype(BF16), jnp.ones((48, 128), BF16), preferred_element_type=F32)


def column_weights(ctap_ref, shifts_ref, weights_ref, diag, tile_weights):
    tile_weights[...] = lane_copies(weights_ref[...].astype(F32))
    j = iota((48, 128), 1)
    shift = lane_copies(shifts_ref[1:2, :].astype(F32))
    offset = jnp.clip(j + shift.astype(jnp.int32) - 3, 0, TC - 6) - j
    kept = [ctap_ref[k].astype(F32) for k in range(6)]
    for o in range(-SPAN, SPAN + 1):
        total = jnp.zeros((48, 128), F32)
        for k in range(6):
            total = jnp.where(offset + k == o, kept[k], total)
        diag[o + SPAN] = total


def row_weights(rtap_ref, rowtaps):
    for k in range(6):
        taps = rtap_ref[k].astype(F32).T
        rowtaps[k] = jnp.concatenate(
            [taps[0:16], taps[16:32], taps[32:48], jnp.zeros((16, 56), F32)], axis=1
        )


def row_warp(p0, p1, shifts_s, rowtaps, half):
    lane1 = iota((1, 128), 1)
    third_of, row_of = lane1 // TR, lane1 % TR
    rr = iota((72, 128), 0)

    def trio(n, carry):
        at = pl.ds(pl.multiple_of(n * TR, 8), TR)
        left, right = p0[at, :], p1[at, :]
        stack = jnp.concatenate(
            [left[:, :128], left[:, 128:] + right[:, :128], right[:, 128:]], axis=0
        ).astype(BF16)
        shift = jnp.where(
            third_of == 0,
            shifts_s[0, n],
            jnp.where(third_of == 1, shifts_s[0, n + 16], shifts_s[0, n + 32]),
        )
        base = third_of * TR + jnp.clip(row_of + shift - 3, 0, TR - 6)
        delta = rr - jnp.broadcast_to(base, (72, 128))
        band = jnp.zeros((72, 128), F32)
        for k in range(6):
            taps = jnp.broadcast_to(rowtaps[k, pl.ds(n, 1), :], (72, 128))
            band = jnp.where(delta == k, taps, band)
        out = lax.dot_general(
            band.astype(BF16), stack, (((0,), (0,)), ((), ())), preferred_element_type=F32
        )
        half[n] = out[:72]
        return carry

    lax.fori_loop(0, TRIOS, trio, 0, unroll=UNROLL_A)


def place_tiles(half, words_s, dest_s, slot_s, diag, tile_weights, count, blocks):
    bit = 8 * (iota((TR, 128), 0) // 6) + iota((TR, 128), 1) // 16
    lane1 = iota((1, 128), 1)

    def trio(n, carry):
        for third in range(3):
            t = n + 16 * third
            h = half[n, pl.ds(TR * third, TR), :]
            acc = jnp.broadcast_to(diag[SPAN, pl.ds(t, 1), :], (TR, 128)) * h
            for o in range(1, SPAN + 1):
                for sign in (-o, o):
                    d = jnp.broadcast_to(diag[sign + SPAN, pl.ds(t, 1), :], (TR, 128))
                    acc = acc + d * pltpu.roll(h, (-sign) % 128, 1)
            word, weight = words_s[t], tile_weights[pl.ds(t, 1), :]
            flagged = lax.shift_right_logical(jnp.full((TR, 128), word, jnp.int32), bit) & 1
            prod = acc * jnp.where(flagged == 0, jnp.broadcast_to(weight, (TR, 128)), 0.0)
            to = dest_s[0, t]
            rank = count[to]
            count[to] = rank + 1
            at = 2 * to + rank
            blocks[pl.ds(at, TR, stride=PITCH), :] = prod
            flag1 = lax.shift_right_logical(jnp.full((1, 128), word, jnp.int32), lane1 & 31) & 1
            blocks[pl.ds(TR * PITCH + at, 1), :] = jnp.where(
                lane1 < 32,
                jnp.where(flag1 == 0, weight, 0.0),
                jnp.where(lane1 == 32, jnp.full((1, 128), slot_s[t], jnp.int32).astype(F32), 0.0),
            )
        return carry

    lax.fori_loop(0, TRIOS, trio, 0, unroll=UNROLL_B)


def clear_blocks(count, blocks):
    blocks[...] = jnp.zeros(blocks.shape, F32)

    def clear(d, carry):
        count[d] = 0
        return carry

    lax.fori_loop(0, 64, clear, 0, unroll=8)


def send_kernel(
    words_s,
    dest_s,
    slot_s,
    shifts_s,
    coef_s,
    shifts_ref,
    weights_ref,
    rtap_ref,
    ctap_ref,
    brow_ref,
    bcol_ref,
    tiles_hbm,
    out_ref,
    tiles,
    sems,
    flat,
    image,
    pad,
    rtab,
    w0,
    w1,
    s0,
    s1,
    p0,
    p1,
    rowtaps,
    diag,
    half,
    tile_weights,
    blocks,
    count,
):
    copies = []
    for octet in range(6):
        rows = pl.ds(8 * octet, 8)
        copies.append(
            pltpu.make_async_copy(tiles_hbm.at[rows, :], tiles.at[rows, :], sems.at[octet])
        )
        copies[-1].start()
    make_tables(brow_ref, bcol_ref, pad, rtab, w0, w1)
    column_weights(ctap_ref, shifts_ref, weights_ref, diag, tile_weights)
    row_weights(rtap_ref, rowtaps)
    clear_blocks(count, blocks)
    unpack_tiles(tiles, copies, flat, image)
    row_stage(image, rtab, coef_s, s0, s1)
    p0[...] = jnp.dot(s0[...], w0[...], preferred_element_type=F32)
    p1[...] = jnp.dot(s1[...], w1[...], preferred_element_type=F32)
    row_warp(p0, p1, shifts_s, rowtaps, half)
    place_tiles(half, words_s, dest_s, slot_s, diag, tile_weights, count, blocks)
    for i in range(TR + 1):
        out_ref[:, pl.ds(128 * i, 128)] = blocks[pl.ds(PITCH * i, 128), :].astype(BF16)


UNROLL_A = 8
UNROLL_B = 4


def send_blocks(tiles, coef, rtap, ctap, shifts, words, weights, dest, slot, brow, bcol):
    smem = pl.BlockSpec(memory_space=pltpu.SMEM)
    vmem = pl.BlockSpec(memory_space=pltpu.VMEM)
    return pl.pallas_call(
        send_kernel,
        out_shape=pltpu.VMEM((128, (TR + 1) * 128), BF16),
        in_specs=[smem] * 5 + [vmem] * 6 + [pl.BlockSpec(memory_space=pltpu.HBM)],
        out_specs=vmem,
        scratch_shapes=[
            pltpu.VMEM((48, IR * IC), BF16),
            pltpu.SemaphoreType.DMA((6,)),
            pltpu.VMEM((48 * 84 + 8, 128), F32),
            pltpu.VMEM((4 * TRIOS * IR, 128), F32),
            pltpu.VMEM((32, 128), F32),
            pltpu.VMEM((NB * TR, 128), F32),
            pltpu.VMEM((NB * 256, 256), BF16),
            pltpu.VMEM((NB * 256, 256), BF16),
            pltpu.VMEM((384, NB * 256), BF16),
            pltpu.VMEM((384, NB * 256), BF16),
            pltpu.VMEM((384, 256), F32),
            pltpu.VMEM((384, 256), F32),
            pltpu.VMEM((6, TRIOS, 128), F32),
            pltpu.VMEM((2 * SPAN + 1, 48, 128), F32),
            pltpu.VMEM((TRIOS, 72, 128), F32),
            pltpu.VMEM((48, 128), F32),
            pltpu.VMEM(((TR + 1) * PITCH, 128), F32),
            pltpu.SMEM((64,), jnp.int32),
        ],
        compiler_params=pltpu.CompilerParams(vmem_limit_bytes=65994752),
        name="match_and_warp",
    )(
        words,
        dest.T,
        slot,
        shifts.T,
        coef.T,
        shifts.T,
        weights.reshape(1, 48),
        rtap.transpose(1, 2, 0),
        ctap.transpose(1, 0, 2),
        brow,
        bcol,
        tiles,
    )


def body(
    padded_tiles,
    coefficients,
    row_taps,
    col_taps,
    shifts,
    mask_words,
    weights,
    destination,
    patch_slot,
    basis_rows,
    basis_cols,
):
    blocks = send_blocks(
        padded_tiles,
        coefficients,
        row_taps,
        col_taps,
        shifts,
        mask_words,
        weights,
        destination,
        patch_slot,
        basis_rows,
        basis_cols,
    )
    send = blocks.reshape(64, 2, TR * TC + 128)
    recv = lax.all_to_all(send, "sky", split_axis=0, concat_axis=0, tiled=True)
    recv = recv.reshape(128, TR * TC + 128)
    slot_of = recv[:, TR * TC + 32].astype(jnp.int32)
    pick = (iota((16, 128), 0) == slot_of[None, :]).astype(BF16)
    sums = jnp.dot(pick, recv, preferred_element_type=F32).astype(BF16)
    parts = sums.reshape(8, 2, TR * TC + 128)
    parts = lax.all_to_all(parts, "exp", split_axis=0, concat_axis=0, tiled=True)
    totals = jnp.sum(parts.astype(F32), axis=0)
    numerator = totals[:, : TR * TC].reshape(2 * TR, TC)
    weight_sum = spread_cells(totals[:, TR * TC : TR * TC + 32]).reshape(2 * TR, TC)
    return numerator / jnp.maximum(weight_sum, 1.0)


def spread_cells(cells):
    grid = jnp.repeat(cells.reshape(2, 4, 8), TR // 4, axis=1)
    return jnp.repeat(grid, TC // 8, axis=2)


def solution(mesh):
    placed = (
        P(("sky", "exp"), None),
        P(("sky", "exp"), None),
        P(("sky", "exp"), None, None),
        P(("sky", "exp"), None, None),
        P(("sky", "exp"), None),
        P(("sky", "exp")),
        P(("sky", "exp")),
        P(("sky", "exp"), None),
        P(("sky", "exp")),
        P(),
        P(),
    )
    return jax.shard_map(
        body, mesh=mesh, in_specs=placed, out_specs=P(("sky", "exp"), None), check_vma=False
    )
```

```python
import jax
import jax.numpy as jnp
from jax import lax
from jax.experimental import pallas as pl
from jax.experimental.pallas import tpu as pltpu
from jax.sharding import PartitionSpec as P

F32 = jnp.float32
BF16 = jnp.bfloat16
TRIOS = 16
NB = 20
KW = 41
TR = 24
TC = 128
IR = TR + KW - 1
IC = TC + KW - 1
SPAN = 5
PITCH = 136


def iota(shape, axis):
    return lax.broadcasted_iota(jnp.int32, shape, axis)


def unpack_tiles(tiles_ref, copies, flat, image):
    for octet in range(6):
        copies[octet].wait()
        for p in range(84):
            block = tiles_ref[pl.ds(8 * octet, 8), pl.ds(128 * p, 128)].astype(F32)
            flat[pl.ds(8 * octet * 84 + p, 8, stride=84), :] = block
    lane = iota((64, 128), 1)
    for m in range(16):
        first, rest = divmod(IC * m, 128)
        parts = [None] * 4
        for third in range(3):
            shift = (rest - IC * third) % 128
            base = third * 16 * 84 + first
            rolled = {}

            def row(q, rolled=rolled, base=base, shift=shift):
                if q not in rolled:
                    val = flat[pl.ds(base + q, 64, stride=21), :]
                    rolled[q] = pltpu.roll(val, (128 - shift) % 128, 1) if shift else val
                return rolled[q]

            for d in range(4):
                lo, hi = max(128 * d, IC * third), min(128 * d + 128, IC * third + IC)
                if lo >= hi:
                    continue
                start = rest - IC * third + 128 * d
                q0 = start // 128
                edge = 128 - start % 128
                l0, l1 = lo - 128 * d, hi - 128 * d
                if l1 <= edge:
                    val = row(q0)
                elif l0 >= edge:
                    val = row(q0 + 1)
                else:
                    val = jnp.where(lane < edge, row(q0), row(q0 + 1))
                if parts[d] is None:
                    parts[d] = val if l1 == 128 else jnp.where(lane < l1, val, 0.0)
                else:
                    parts[d] = jnp.where(lane < l0, parts[d], val if l1 == 128 else jnp.where(lane < l1, val, 0.0))
        for d in range(4):
            image[pl.ds(d * TRIOS * IR + m, 64, stride=16), :] = parts[d]


def make_tables(brow_ref, bcol_ref, pad, rtab, w0, w1):
    pad[...] = jnp.zeros((32, 128), F32)
    pad[0:NB, 0:KW] = brow_ref[...].astype(F32)
    for b in range(NB):
        line = jnp.broadcast_to(pad[pl.ds(b, 1), :], (TR, 128))
        line = pltpu.roll(line, 0, 1, stride=1, stride_axis=0)
        rtab[pl.ds(b * TR, TR), :] = line
    pad[0:NB, 0:KW] = bcol_ref[...].astype(F32)
    mirror = ((iota((128, 128), 0) + iota((128, 128), 1)) % 128 == 0).astype(BF16)
    rev = jnp.dot(pad[...].astype(BF16), mirror, preferred_element_type=F32)
    pad[...] = rev
    gap = iota((IC, 128), 0) - iota((IC, 128), 1)
    inside = (gap >= 0) & (gap < KW)
    for b in range(NB):
        line = jnp.broadcast_to(pad[pl.ds(b, 1), :], (128, 128))
        line = pltpu.roll(line, 0, 1, stride=1, stride_axis=0)
        band = jnp.concatenate([line, line[: IC - 128]], axis=0)
        band = jnp.where(inside, band, 0.0)
        zero = jnp.zeros((176, 128), F32)
        r = pl.ds(b * 256, 256)
        w0[r, 0:128] = jnp.concatenate([band, zero[:88]], axis=0).astype(BF16)
        w0[r, 128:256] = jnp.concatenate([zero[:168], band[:88]], axis=0).astype(BF16)
        w1[r, 0:128] = jnp.concatenate([band[88:168], zero[:176]], axis=0).astype(BF16)
        w1[r, 128:256] = jnp.concatenate([zero[:80], band, zero[:8]], axis=0).astype(BF16)


def row_stage(image, rtab, coef_s, s0, s1):
    table = rtab[...].astype(BF16)[:, :IR]
    lane = iota((8, 512), 1)

    def step(u, carry):
        halves = []
        for h in range(2):
            n = 2 * u + h
            x = jnp.concatenate(
                [image[pl.ds(pl.multiple_of(d * TRIOS * IR + n * IR, 8), IR), :] for d in range(4)],
                axis=1,
            ).astype(BF16)
            halves.append((n, jnp.dot(table, x, preferred_element_type=F32)))
        for b in range(NB):
            rows = []
            for n, rp in halves:
                scale = jnp.where(
                    lane < IC,
                    coef_s[b, n],
                    jnp.where(lane < 2 * IC, coef_s[b, n + 16], coef_s[b, n + 32]),
                )
                for a in range(3):
                    k = b * TR + 8 * a
                    rows.append(rp[k : k + 8] * scale)
            block = jnp.concatenate(rows, axis=0).astype(BF16)
            at = pl.ds(pl.multiple_of(48 * u, 16), 48)
            s0[at, pl.ds(b * 256, 256)] = block[:, :256]
            s1[at, pl.ds(b * 256, 256)] = block[:, 256:]
        return carry

    lax.fori_loop(0, TRIOS // 2, step, 0)


def lane_copies(row):
    own = jnp.where(
        iota((48, 48), 0) == iota((48, 48), 1), jnp.broadcast_to(row, (48, 48)), 0.0
    )
    return jnp.dot(own.astype(BF16), jnp.ones((48, 128), BF16), preferred_element_type=F32)


def column_weights(ctap_ref, shifts_ref, weights_ref, diag, tile_weights):
    tile_weights[...] = lane_copies(weights_ref[...].astype(F32))
    j = iota((48, 128), 1)
    shift = lane_copies(shifts_ref[1:2, :].astype(F32))
    offset = jnp.clip(j + shift.astype(jnp.int32) - 3, 0, TC - 6) - j
    kept = [ctap_ref[k].astype(F32) for k in range(6)]
    for o in range(-SPAN, SPAN + 1):
        total = jnp.zeros((48, 128), F32)
        for k in range(6):
            total = jnp.where(offset + k == o, kept[k], total)
        diag[o + SPAN] = total


def row_weights(rtap_ref, rowtaps):
    for k in range(6):
        taps = rtap_ref[k].astype(F32).T
        rowtaps[k] = jnp.concatenate(
            [taps[0:16], taps[16:32], taps[32:48], jnp.zeros((16, 56), F32)], axis=1
        )


def row_warp(p0, p1, shifts_s, rowtaps, half):
    lane1 = iota((1, 128), 1)
    third_of, row_of = lane1 // TR, lane1 % TR
    rr = iota((72, 128), 0)

    def trio(n, carry):
        at = pl.ds(pl.multiple_of(n * TR, 8), TR)
        left, right = p0[at, :], p1[at, :]
        stack = jnp.concatenate(
            [left[:, :128], left[:, 128:] + right[:, :128], right[:, 128:]], axis=0
        ).astype(BF16)
        shift = jnp.where(
            third_of == 0,
            shifts_s[0, n],
            jnp.where(third_of == 1, shifts_s[0, n + 16], shifts_s[0, n + 32]),
        )
        base = third_of * TR + jnp.clip(row_of + shift - 3, 0, TR - 6)
        delta = rr - jnp.broadcast_to(base, (72, 128))
        band = jnp.zeros((72, 128), F32)
        for k in range(6):
            taps = jnp.broadcast_to(rowtaps[k, pl.ds(n, 1), :], (72, 128))
            band = jnp.where(delta == k, taps, band)
        out = lax.dot_general(
            band.astype(BF16), stack, (((0,), (0,)), ((), ())), preferred_element_type=F32
        )
        half[n] = out[:72]
        return carry

    lax.fori_loop(0, TRIOS, trio, 0, unroll=UNROLL_A)


def place_tiles(half, words_s, dest_s, slot_s, diag, tile_weights, count, blocks):
    bit = 8 * (iota((TR, 128), 0) // 6) + iota((TR, 128), 1) // 16
    lane1 = iota((1, 128), 1)

    def trio(n, carry):
        for third in range(3):
            t = n + 16 * third
            h = half[n, pl.ds(TR * third, TR), :]
            acc = jnp.broadcast_to(diag[SPAN, pl.ds(t, 1), :], (TR, 128)) * h
            for o in range(1, SPAN + 1):
                for sign in (-o, o):
                    d = jnp.broadcast_to(diag[sign + SPAN, pl.ds(t, 1), :], (TR, 128))
                    acc = acc + d * pltpu.roll(h, (-sign) % 128, 1)
            word, weight = words_s[t], tile_weights[pl.ds(t, 1), :]
            flagged = lax.shift_right_logical(jnp.full((TR, 128), word, jnp.int32), bit) & 1
            prod = acc * jnp.where(flagged == 0, jnp.broadcast_to(weight, (TR, 128)), 0.0)
            to = dest_s[0, t]
            rank = count[to]
            count[to] = rank + 1
            at = 2 * to + rank
            blocks[pl.ds(at, TR, stride=PITCH), :] = prod
            flag1 = lax.shift_right_logical(jnp.full((1, 128), word, jnp.int32), lane1 & 31) & 1
            blocks[pl.ds(TR * PITCH + at, 1), :] = jnp.where(
                lane1 < 32,
                jnp.where(flag1 == 0, weight, 0.0),
                jnp.where(lane1 == 32, jnp.full((1, 128), slot_s[t], jnp.int32).astype(F32), 0.0),
            )
        return carry

    lax.fori_loop(0, TRIOS, trio, 0, unroll=UNROLL_B)


def clear_blocks(count, blocks):
    blocks[...] = jnp.zeros(blocks.shape, F32)

    def clear(d, carry):
        count[d] = 0
        return carry

    lax.fori_loop(0, 64, clear, 0, unroll=8)


def send_kernel(
    words_s,
    dest_s,
    slot_s,
    shifts_s,
    coef_s,
    shifts_ref,
    weights_ref,
    rtap_ref,
    ctap_ref,
    brow_ref,
    bcol_ref,
    tiles_hbm,
    out_ref,
    tiles,
    sems,
    flat,
    image,
    pad,
    rtab,
    w0,
    w1,
    s0,
    s1,
    p0,
    p1,
    rowtaps,
    diag,
    half,
    tile_weights,
    blocks,
    count,
):
    copies = []
    for octet in range(6):
        rows = pl.ds(8 * octet, 8)
        copies.append(
            pltpu.make_async_copy(tiles_hbm.at[rows, :], tiles.at[rows, :], sems.at[octet])
        )
        copies[-1].start()
    make_tables(brow_ref, bcol_ref, pad, rtab, w0, w1)
    column_weights(ctap_ref, shifts_ref, weights_ref, diag, tile_weights)
    row_weights(rtap_ref, rowtaps)
    clear_blocks(count, blocks)
    unpack_tiles(tiles, copies, flat, image)
    row_stage(image, rtab, coef_s, s0, s1)
    p0[...] = jnp.dot(s0[...], w0[...], preferred_element_type=F32)
    p1[...] = jnp.dot(s1[...], w1[...], preferred_element_type=F32)
    row_warp(p0, p1, shifts_s, rowtaps, half)
    place_tiles(half, words_s, dest_s, slot_s, diag, tile_weights, count, blocks)
    for i in range(TR + 1):
        out_ref[:, pl.ds(128 * i, 128)] = blocks[pl.ds(PITCH * i, 128), :].astype(BF16)


UNROLL_A = 16
UNROLL_B = 4


def send_blocks(tiles, coef, rtap, ctap, shifts, words, weights, dest, slot, brow, bcol):
    smem = pl.BlockSpec(memory_space=pltpu.SMEM)
    vmem = pl.BlockSpec(memory_space=pltpu.VMEM)
    return pl.pallas_call(
        send_kernel,
        out_shape=pltpu.VMEM((128, (TR + 1) * 128), BF16),
        in_specs=[smem] * 5 + [vmem] * 6 + [pl.BlockSpec(memory_space=pltpu.HBM)],
        out_specs=vmem,
        scratch_shapes=[
            pltpu.VMEM((48, IR * IC), BF16),
            pltpu.SemaphoreType.DMA((6,)),
            pltpu.VMEM((48 * 84 + 96, 128), F32),
            pltpu.VMEM((4 * TRIOS * IR + 16, 128), F32),
            pltpu.VMEM((32, 128), F32),
            pltpu.VMEM((NB * TR, 128), F32),
            pltpu.VMEM((NB * 256, 256), BF16),
            pltpu.VMEM((NB * 256, 256), BF16),
            pltpu.VMEM((384, NB * 256), BF16),
            pltpu.VMEM((384, NB * 256), BF16),
            pltpu.VMEM((384, 256), F32),
            pltpu.VMEM((384, 256), F32),
            pltpu.VMEM((6, TRIOS, 128), F32),
            pltpu.VMEM((2 * SPAN + 1, 48, 128), F32),
            pltpu.VMEM((TRIOS, 72, 128), F32),
            pltpu.VMEM((48, 128), F32),
            pltpu.VMEM(((TR + 2) * PITCH, 128), F32),
            pltpu.SMEM((64,), jnp.int32),
        ],
        compiler_params=pltpu.CompilerParams(vmem_limit_bytes=65994752),
        name="match_and_warp",
    )(
        words,
        dest.T,
        slot,
        shifts.T,
        coef.T,
        shifts.T,
        weights.reshape(1, 48),
        rtap.transpose(1, 2, 0),
        ctap.transpose(1, 0, 2),
        brow,
        bcol,
        tiles,
    )


def body(
    padded_tiles,
    coefficients,
    row_taps,
    col_taps,
    shifts,
    mask_words,
    weights,
    destination,
    patch_slot,
    basis_rows,
    basis_cols,
):
    blocks = send_blocks(
        padded_tiles,
        coefficients,
        row_taps,
        col_taps,
        shifts,
        mask_words,
        weights,
        destination,
        patch_slot,
        basis_rows,
        basis_cols,
    )
    send = blocks.reshape(64, 2, TR * TC + 128)
    recv = lax.all_to_all(send, "sky", split_axis=0, concat_axis=0, tiled=True)
    recv = recv.reshape(128, TR * TC + 128)
    slot_of = recv[:, TR * TC + 32].astype(jnp.int32)
    pick = (iota((16, 128), 0) == slot_of[None, :]).astype(BF16)
    sums = jnp.dot(pick, recv, preferred_element_type=F32).astype(BF16)
    parts = sums.reshape(8, 2, TR * TC + 128)
    parts = lax.all_to_all(parts, "exp", split_axis=0, concat_axis=0, tiled=True)
    totals = jnp.sum(parts.astype(F32), axis=0)
    numerator = totals[:, : TR * TC].reshape(2 * TR, TC)
    weight_sum = spread_cells(totals[:, TR * TC : TR * TC + 32]).reshape(2 * TR, TC)
    return numerator / jnp.maximum(weight_sum, 1.0)


def spread_cells(cells):
    grid = jnp.repeat(cells.reshape(2, 4, 8), TR // 4, axis=1)
    return jnp.repeat(grid, TC // 8, axis=2)


def solution(mesh):
    placed = (
        P(("sky", "exp"), None),
        P(("sky", "exp"), None),
        P(("sky", "exp"), None, None),
        P(("sky", "exp"), None, None),
        P(("sky", "exp"), None),
        P(("sky", "exp")),
        P(("sky", "exp")),
        P(("sky", "exp"), None),
        P(("sky", "exp")),
        P(),
        P(),
    )
    return jax.shard_map(
        body, mesh=mesh, in_specs=placed, out_specs=P(("sky", "exp"), None), check_vma=False
    )
```
